32 devices in a mesh: chan: 2 (over x), ctx: 16 (over z, y, core).
Axes of the slice: x: 2, y: 2, z: 4, core: 2. Of those that a mesh axis runs over, the one named last changes fastest.
Arguments:
- value: bfloat16 [2, 2048, 2048], P(None, 'ctx', 'chan'), may hold values from -6 to 6
- gate_in: bfloat16 [2, 2048, 2048], P(None, 'ctx', 'chan'), may hold values from -6 to 6
- gate_out: bfloat16 [2, 2048, 2048], P(None, 'ctx', 'chan'), may hold values from -6 to 6
- filters: float32 [384, 2048], P(None, 'chan'), may hold values from -0.3125 to 0.3125
- skip: float32 [2048], P('chan'), may hold values from -5 to 5
- proj: bfloat16 [2048, 2048], P(('chan', 'ctx')), may hold values from -0.125 to 0.125
- taps: float32 [128, 2048], P(None, 'chan'), may hold values from -0.5 to 0.5
Outputs:
- result: bfloat16 [2, 2048, 2048], P(None, 'ctx', 'chan')
The draws below stay inside these ranges and needn't reach their ends.
All inputs are finite; a program needn't handle non-finite values.
Results may differ from the reference program's by a relative error of at most 0.0057.
Values may be sent and summed in bfloat16 or wider, within the bound.
A program may use at most 128 MiB of HBM per device.

```python
import jax
import jax.numpy as jnp
from jax import lax

D = 2048
BATCH = 2
SHORT = 128
LENGTH = 2048
LAGS = 384
N_CHAN = 2


def level_of(rng, dims, cuts, least, largest):
    def one(dim, shards_of):
        heights = jax.random.uniform(jax.random.fold_in(jax.random.fold_in(rng, 6), dim), (shards_of,), jnp.float32, least / len(cuts), largest / len(cuts))
        return jnp.repeat(jnp.exp(heights), dims[dim] // shards_of).reshape((-1,) + (1,) * (len(dims) - dim - 1))

    level = one(*cuts[0])
    for cut in cuts[1:]:
        level = level * one(*cut)
    return level


def normal_values(rng, shape, width, limit, cuts=(), dtype=jnp.bfloat16):
    drawn = width * jax.random.normal(rng, shape, jnp.float32)
    if cuts:
        drawn = drawn * level_of(rng, shape, cuts, -0.22, 0.18)
    return jnp.clip(drawn, -limit, limit).astype(dtype)


def setup_inputs(seed: int = 0) -> dict:
    key_list = jax.random.split(jax.random.key(seed), 8)
    value = normal_values(key_list[0], (BATCH, LENGTH, D), 1.0, 6.0, ((1, 16), (2, 2)))
    gate_in = normal_values(key_list[1], (BATCH, LENGTH, D), 1.0, 6.0, ((1, 16), (2, 2)))
    gate_out = normal_values(key_list[2], (BATCH, LENGTH, D), 1.0, 6.0, ((1, 16), (2, 2)))
    filters = normal_values(key_list[3], (LAGS, D), LAGS ** -0.5, 0.3125, ((1, 2),), jnp.float32)
    skip = normal_values(key_list[4], (D,), 1.0, 5.0, ((0, 2),), jnp.float32)
    proj = normal_values(key_list[5], (D, D), D ** -0.5, 0.125, ((0, 32),))
    taps = normal_values(key_list[6], (SHORT, D), SHORT ** -0.5, 0.5, ((1, 2),), jnp.float32)
    return {"value": value, "gate_in": gate_in, "gate_out": gate_out, "filters": filters, "skip": skip, "proj": proj, "taps": taps}


def causal_conv(signal, kernel):
    length_total = 2 * signal.shape[0]
    signal_spec = jnp.fft.rfft(signal, n=length_total, axis=0)
    kernel_spec = jnp.fft.rfft(kernel, n=length_total, axis=0)
    return jnp.fft.irfft(signal_spec * kernel_spec, n=length_total, axis=0)[: signal.shape[0]]


def one_sequence(value, gate_in, gate_out, filters, skip, proj, taps):
    group_width = D // N_CHAN
    value_wide = value.astype(jnp.float32)
    value_groups = value_wide.reshape(LENGTH, N_CHAN, group_width).transpose(1, 0, 2)
    filter_groups = filters.astype(jnp.float32).reshape(LAGS, N_CHAN, group_width).transpose(1, 0, 2)
    conv = lax.map(lambda pair: causal_conv(pair[0], pair[1]), (value_groups, filter_groups))
    conv = conv.transpose(1, 0, 2).reshape(LENGTH, D)
    mixed = (gate_in.astype(jnp.float32) * (conv + skip.astype(jnp.float32)[None, :] * value_wide)).astype(jnp.bfloat16)
    projected = jnp.dot(mixed, proj, preferred_element_type=jnp.float32).astype(jnp.bfloat16)
    proj_groups = projected.astype(jnp.float32).reshape(LENGTH, N_CHAN, group_width).transpose(1, 0, 2)
    tap_groups = taps.astype(jnp.float32).reshape(SHORT, N_CHAN, group_width).transpose(1, 0, 2)
    shorted = lax.map(lambda pair: causal_conv(pair[0], pair[1]), (proj_groups, tap_groups))
    shorted = shorted.transpose(1, 0, 2).reshape(LENGTH, D)
    return (gate_out.astype(jnp.float32) * shorted).astype(jnp.bfloat16)


def reference(value, gate_in, gate_out, filters, skip, proj, taps):
    return lax.map(lambda trio: one_sequence(trio[0], trio[1], trio[2], filters, skip, proj, taps), (value, gate_in, gate_out))
```

```python
import functools
import math

import jax
import jax.numpy as jnp
import numpy as np
from jax import lax
from jax.experimental import pallas as pl
from jax.experimental.pallas import tpu as pltpu
from jax.sharding import PartitionSpec as P

F32 = jnp.float32
BF16 = jnp.bfloat16


def split(x):
    high = x.astype(BF16)
    return high, (x - high.astype(F32)).astype(BF16)


def split_table(table):
    high = table.astype(BF16)
    return high, (table - high.astype(np.float64)).astype(BF16)


def tables(rows):
    size = 2 * rows
    product = (2 * np.arange(rows)[:, None] + 1) * np.arange(size)[None, :] % (2 * size)
    phase = product * (math.pi / size)
    forward = np.concatenate([np.cos(phase), -np.sin(phase)], axis=0)
    inverse = forward[:, rows:].T * (2.0 / size)
    return (*split_table(forward), *split_table(np.ascontiguousarray(inverse)))


def mm(left, right):
    return jnp.dot(left, right, preferred_element_type=F32)


def lag_spectrum(lags, fwd_hi, fwd_lo):
    rows = lags.shape[0]
    high, low = split(lags)
    return mm(fwd_hi[:, :rows], high) + mm(fwd_hi[:, :rows], low) + mm(fwd_lo[:, :rows], high)


def convolve(windows, spectra, table_refs):
    fwd_hi, fwd_lo, inv_hi, inv_lo = table_refs
    total_re = total_im = None
    for window, spectrum in zip(windows, spectra):
        seen = mm(fwd_hi[...], window) + mm(fwd_lo[...], window)
        half = seen.shape[0] // 2
        x_re, x_im, h_re, h_im = seen[:half], seen[half:], spectrum[:half], spectrum[half:]
        re = x_re * h_re - x_im * h_im
        im = x_re * h_im + x_im * h_re
        total_re = re if total_re is None else total_re + re
        total_im = im if total_im is None else total_im + im
    high, low = split(jnp.concatenate([total_re, total_im], axis=0))
    return mm(inv_hi[...], high) + mm(inv_hi[...], low) + mm(inv_lo[...], high)


def mix_kernel(fh, fl, ih, il, filters, skip, gate, *rest):
    blocks, out = rest[:-1], rest[-1]
    batch, rows, _ = out.shape
    count = filters.shape[0] // rows
    spectra = [
        lag_spectrum(filters[s * rows : (s + 1) * rows], fh[...], fl[...]) for s in range(count)
    ]
    for b in range(batch):
        windows = [
            jnp.concatenate([blocks[s + 1][b], blocks[s][b]], axis=0) for s in range(count)
        ]
        conv = convolve(windows, spectra, (fh, fl, ih, il))
        own = blocks[0][b].astype(F32)
        out[b] = (gate[b].astype(F32) * (conv + skip[...] * own)).astype(BF16)


def filter_kernel(fh, fl, ih, il, taps, gate, behind, own, out):
    spectra = [lag_spectrum(taps[...], fh[...], fl[...])]
    for b in range(out.shape[0]):
        window = jnp.concatenate([behind[b], own[b]], axis=0)
        shorted = convolve([window], spectra, (fh, fl, ih, il))
        out[b] = (gate[b].astype(F32) * shorted).astype(BF16)


def tiled(kernel, consts, rows_args, block_args, tile, flops):
    batch, rows, channels = block_args[0].shape
    whole = lambda a: pl.BlockSpec(a.shape, lambda i: (0, 0))
    across = lambda a: pl.BlockSpec((a.shape[0], tile), lambda i: (0, i))
    block = pl.BlockSpec((batch, rows, tile), lambda i: (0, 0, i))
    args = [*consts, *rows_args, *block_args]
    return pl.pallas_call(
        kernel,
        grid=(channels // tile,),
        in_specs=[whole(a) for a in consts]
        + [across(a) for a in rows_args]
        + [block for _ in block_args],
        out_specs=block,
        out_shape=jax.ShapeDtypeStruct((batch, rows, channels), BF16),
        cost_estimate=pl.CostEstimate(
            flops=flops,
            bytes_accessed=sum(a.size * a.dtype.itemsize for a in args),
            transcendentals=0,
        ),
    )(*args)


def from_behind(value, steps):
    count = lax.axis_size("ctx")
    return lax.ppermute(value, "ctx", [(s, s + steps) for s in range(count - steps)])


MESH = pl.DeviceIdType.MESH


UNITS = 4


def fused_kernel(
    value_any, proj_any, fh_any, fl_any, ih_any, il_any, skip_any, filters_any, taps_any,
    gate_in_any, gate_out_any,
    out_any,
    value, fh, fl, ih, il, skip, out,
    past, gathered, mixed, spectra, tap_spectra, filters, taps, gate_in, gate_out,
    own_rows, rim,
    load_sem, store_sem, own_sem, back_send, back_recv, halo_send, halo_recv, relay_send, relay_recv, far_send, far_recv,
    near_send, near_recv, ring_send, ring_recv, share_send, share_recv, first_send, first_recv,
    swap_send, swap_recv, mixed_send, mixed_recv, rim_send, rim_recv,
):
    batch, rows, channels = value.shape
    count = lax.axis_size("ctx")
    chips = count // 2
    evens = chips // 2
    width = gathered.shape[-1]
    tile = min(256, width)
    me, j = lax.axis_index("chan"), lax.axis_index("ctx")
    chip, core = j // 2, j % 2
    sibling = chip * 2 + 1 - core
    partner = 1 - me
    place = jnp.where(chip % 2 == 0, chip // 2, chips - 1 - chip // 2)

    def holder(position):
        position = (position + chips) % chips
        number = jnp.where(position < evens, 2 * position, 2 * (chips - 1 - position) + 1)
        return number * 2 + core

    loads = [
        pltpu.make_async_copy(a, b, load_sem.at[i])
        for i, (a, b) in enumerate(
            [
                (filters_any, filters),
                (taps_any, taps),
                (gate_in_any, gate_in),
                (gate_out_any, gate_out),
                (fh_any, fh),
                (fl_any, fl),
                (ih_any, ih),
                (il_any, il),
                (skip_any, skip),
                (value_any, value),
            ]
        )
    ]
    for load in loads:
        load.start()

    def columns(owner, unit):
        return pl.ds(pl.multiple_of(owner * channels + unit * width, width), width)

    own_copies = [
        pltpu.make_async_copy(proj_any.at[:, columns(me, q)], gathered.at[q, me, j], own_sem.at[q])
        for q in range(UNITS)
    ]
    for copy in own_copies:
        copy.start()

    barrier = pltpu.get_barrier_semaphore()
    following, preceding = holder(place + 1), holder(place - 1)
    expected = 3
    for peer in ((me, following), (me, preceding), (partner, j)):
        pl.semaphore_signal(barrier, inc=1, device_id=peer, device_id_type=MESH)
    for offset in (-3, -2, -1, 1, 2, 3):
        there = (j + offset >= 0) & (j + offset < count)
        expected = expected + there.astype(jnp.int32)

        @pl.when(there)
        def _(offset=offset):
            pl.semaphore_signal(barrier, inc=1, device_id=(me, j + offset), device_id_type=MESH)

    pl.semaphore_wait(barrier, expected)

    def remote(source, target, send_sem, recv_sem, peer):
        return pltpu.make_async_remote_copy(
            src_ref=source,
            dst_ref=target,
            send_sem=send_sem,
            recv_sem=recv_sem,
            device_id=peer,
            device_id_type=MESH,
        )

    def halo(b):
        return remote(value_any.at[b], past.at[1, b], halo_send.at[b], halo_recv.at[b], (me, j + 2))

    def far(b):
        return remote(value_any.at[b], past.at[2, b], far_send.at[b], far_recv.at[b], (me, j + 3))

    def near(b):
        return remote(value_any.at[b], past.at[0, b], near_send.at[b], near_recv.at[b], (me, sibling))

    def relay(b, slot):
        return remote(
            past.at[1, b], past.at[slot, b], relay_send.at[b], relay_recv.at[b], (me, sibling)
        )

    def back(b):
        return remote(past.at[2, b], past.at[1, b], back_send.at[b], back_recv.at[b], (me, j - 1))

    first, second = core == 0, core == 1
    even, odd = chip % 2 == 0, chip % 2 == 1
    has_behind = j >= 2
    sends_halo, gets_halo = (j + 2 < count) & (even | first), (j >= 2) & (odd | first)
    sends_far, gets_far = second & (j + 3 < count), first & (j >= 3)
    sends_back, gets_back = first & odd & (j >= 3), second & even & (j >= 2)

    def start_halo(b):
        @pl.when(sends_far)
        def _():
            far(b).start()

        @pl.when(sends_halo)
        def _():
            halo(b).start()

        @pl.when(first)
        def _():
            near(b).start()

    sent = []

    def begin(copy):
        copy.start()
        sent.append(copy)

    reach = chips // 2

    def swap(unit):
        return remote(
            proj_any.at[:, columns(partner, unit)],
            gathered.at[unit, me, j],
            swap_send.at[unit],
            swap_recv.at[unit],
            (partner, j),
        )

    def piece(unit, direction, step, origin):
        if step < reach:
            return gathered.at[unit, :, origin]
        return gathered.at[unit, 0 if direction == 1 else 1, origin]

    def slot(direction, step):
        return step - 1 if direction == 1 else reach + step - 1

    def hop(unit, direction, step):
        origin = holder(place - direction * (step - 1))
        k = slot(direction, step)
        moved = piece(unit, direction, step, origin)
        return remote(
            moved,
            moved,
            ring_send.at[unit, k],
            ring_recv.at[unit, k],
            (me, following if direction == 1 else preceding),
        )

    def share(unit, direction, step, other=False):
        origin = holder(place - direction * step)
        if other:
            origin = origin + 1 - 2 * core
        k = slot(direction, step)
        moved = piece(unit, direction, step, origin)
        return remote(
            moved, moved, share_send.at[unit, k], share_recv.at[unit, k], (me, sibling)
        )

    def share_own(unit, other=False):
        moved = gathered.at[unit, :, sibling if other else j]
        return remote(moved, moved, first_send.at[unit], first_recv.at[unit], (me, sibling))

    hops = {}

    def wave(unit, step):
        if step == 1:
            own_copies[unit].wait()
            swaps[unit].wait_recv()
        for direction in (1, -1):
            if step > 1:
                hops[unit, direction, step - 1].wait_recv()
            if step <= reach:
                copy = hops[unit, direction, step] = hop(unit, direction, step)
                begin(copy)
        if step == 1:
            begin(share_own(unit))
        else:
            for direction in (1, -1):
                begin(share(unit, direction, step - 1))

    def finish(unit):
        share_own(unit, other=True).wait_recv()
        for direction in (1, -1):
            for step in range(1, reach + 1):
                share(unit, direction, step, other=True).wait_recv()

    def product(unit):
        total = None
        for plane in range(2):
            table = gathered[unit, plane].reshape(count * proj_any.shape[0], width)
            part = mm(mixed[plane].reshape(batch * rows, channels), table)
            total = part if total is None else total + part
        return total

    swaps = [swap(unit) for unit in range(UNITS)]
    for copy in swaps:
        begin(copy)
    start_halo(0)
    wave(0, 1)
    wave(1, 1)
    start_halo(1)
    wave(2, 1)
    wave(3, 1)
    waves = [(unit, step) for step in range(2, reach + 2) for unit in range(UNITS)]

    def pump(number):
        for _ in range(number):
            if waves:
                wave(*waves.pop(0))

    table_refs = (fh, fl, ih, il)
    for load in (loads[0], *loads[4:]):
        load.wait()

    @pl.loop(0, channels // tile)
    def _(i):
        at = pl.ds(pl.multiple_of(i * tile, tile), tile)
        for s in range(spectra.shape[0]):
            spectra[s, :, at] = lag_spectrum(filters[s * rows : (s + 1) * rows, at], fh[...], fl[...])

    @pl.when(j < 2)
    def _():
        past[1] = jnp.zeros(past.shape[1:], BF16)

    @pl.when((j < 2) & first)
    def _():
        past[0] = jnp.zeros(past.shape[1:], BF16)

    @pl.when((j < 2) & second | (j < 3) & first)
    def _():
        past[2] = jnp.zeros(past.shape[1:], BF16)

    def relay_halo(b):
        @pl.when(gets_far)
        def _():
            far(b).wait_recv()

        @pl.when(sends_back)
        def _():
            back(b).start()

        @pl.when(gets_halo)
        def _():
            halo(b).wait_recv()

        @pl.when(gets_back)
        def _():
            back(b).wait_recv()

        @pl.when(has_behind & first)
        def _():
            relay(b, 2).start()

        @pl.when(has_behind & second)
        def _():
            relay(b, 0).start()

    relay_halo(0)
    pump(2)
    relay_halo(1)
    pump(2)
    loads[2].wait()

    def mix(b):
        @pl.when(second)
        def _():
            near(b).wait_recv()

        @pl.when(has_behind & first)
        def _():
            relay(b, 0).wait_recv()

        @pl.when(has_behind & second)
        def _():
            relay(b, 2).wait_recv()

        @pl.loop(0, channels // tile)
        def _(i):
            at = pl.ds(pl.multiple_of(i * tile, tile), tile)
            parts = [value[b, :, at]] + [past[s, b, :, at] for s in range(3)]
            windows = [jnp.concatenate([parts[s + 1], parts[s]], axis=0) for s in range(3)]
            conv = convolve(windows, [spectra.at[s, :, at][...] for s in range(3)], table_refs)
            both = conv + skip[:, at] * parts[0].astype(F32)
            gated = gate_in[b, :, at].astype(F32) * both
            mixed[me, b, :, at] = gated.astype(BF16)

    def trade(b):
        return remote(
            mixed.at[me, b], mixed.at[me, b], mixed_send.at[b], mixed_recv.at[b], (partner, j)
        )

    def traded(b):
        moved = mixed.at[partner, b]
        return remote(moved, moved, mixed_send.at[b], mixed_recv.at[b], (partner, j))

    mix(0)
    begin(trade(0))
    pump(2)
    mix(1)
    begin(trade(1))
    pump(4)
    loads[1].wait()

    @pl.loop(0, channels // tile)
    def _(i):
        at = pl.ds(pl.multiple_of(i * tile, tile), tile)
        tap_spectra[:, at] = lag_spectrum(taps[:, at], fh[...], fl[...])

    @pl.when(j == 0)
    def _():
        rim[...] = jnp.zeros(rim.shape, BF16)

    loads[3].wait()

    def edge(u):
        return remote(
            own_rows.at[u], rim.at[u], rim_send.at[u], rim_recv.at[u], (me, j + 1)
        )

    def store(u):
        part = pl.ds(u * width, width)
        return pltpu.make_async_copy(
            out.at[:, :, part], out_any.at[:, :, part], store_sem.at[u]
        )

    def emit(u):
        @pl.when(j >= 1)
        def _():
            edge(u).wait_recv()

        wide = pl.ds(u * width, width)
        spectrum = tap_spectra[:, wide]
        for b in range(batch):
            window = jnp.concatenate([rim[u, b], own_rows[u, b]], axis=0)
            shorted = convolve([window], [spectrum], table_refs)
            out[b, :, wide] = (gate_out[b, :, wide].astype(F32) * shorted).astype(BF16)
        store(u).start()

    for u in range(UNITS):
        while any(w[0] == u for w in waves):
            pump(1)
        finish(u)
        if u == 0:
            for b in range(batch):
                traded(b).wait_recv()
        own_rows[u] = product(u).astype(BF16).reshape(batch, rows, width)

        @pl.when(j + 1 < count)
        def _(u=u):
            edge(u).start()

        if u:
            emit(u - 1)
    emit(UNITS - 1)

    for u in range(UNITS):
        store(u).wait()
    for copy in sent:
        copy.wait_send()

    for b in range(batch):

        @pl.when(sends_halo)
        def _(b=b):
            halo(b).wait_send()

        @pl.when(first)
        def _(b=b):
            near(b).wait_send()

        @pl.when(sends_far)
        def _(b=b):
            far(b).wait_send()

        @pl.when(has_behind)
        def _(b=b):
            relay(b, 0).wait_send()

        @pl.when(sends_back)
        def _(b=b):
            back(b).wait_send()

    for u in range(UNITS):

        @pl.when(j + 1 < count)
        def _(u=u):
            edge(u).wait_send()


def fused(value, gate_in, gate_out, filters, skip, proj, taps):
    batch, rows, channels = value.shape
    count = lax.axis_size("ctx")
    consts = [jnp.asarray(t) for t in tables(rows)]
    width = channels // UNITS
    slots = 2 * (count // 4)
    dma = pltpu.SemaphoreType.DMA
    anywhere = pl.BlockSpec(memory_space=pl.ANY)
    return pl.pallas_call(
        fused_kernel,
        out_shape=jax.ShapeDtypeStruct(value.shape, BF16),
        in_specs=[anywhere] * 11,
        out_specs=anywhere,
        scratch_shapes=[
            pltpu.VMEM(value.shape, BF16),
            *(pltpu.VMEM(t.shape, BF16) for t in consts),
            pltpu.VMEM((1, channels), F32),
            pltpu.VMEM(value.shape, BF16),
            pltpu.VMEM((3, batch, rows, channels), BF16),
            pltpu.VMEM((UNITS, 2, count, proj.shape[0], width), BF16),
            pltpu.VMEM((2, batch, rows, channels), BF16),
            pltpu.VMEM((3, 2 * rows, channels), F32),
            pltpu.VMEM((2 * rows, channels), F32),
            pltpu.VMEM(filters.shape, F32),
            pltpu.VMEM(taps.shape, F32),
            pltpu.VMEM(value.shape, BF16),
            pltpu.VMEM(value.shape, BF16),
            pltpu.VMEM((UNITS, batch, rows, width), BF16),
            pltpu.VMEM((UNITS, batch, rows, width), BF16),
            dma((10,)),
            dma((UNITS,)),
            dma((UNITS,)),
            dma((batch,)),
            dma((batch,)),
        ]
        + [dma((batch,))] * 8
        + [dma((UNITS, slots))] * 4
        + [dma((UNITS,))] * 4
        + [dma((batch,))] * 2
        + [dma((UNITS,))] * 2,
        compiler_params=pltpu.CompilerParams(
            collective_id=0, has_side_effects=True, vmem_limit_bytes=67043328
        ),
    )(value, proj, *consts, skip[None], filters, taps, gate_in, gate_out)


def per_device(value, gate_in, gate_out, filters, skip, proj, taps):
    batch, rows, channels = value.shape
    assert filters.shape[0] % rows == 0 and taps.shape[0] <= rows
    count = filters.shape[0] // rows
    if (
        lax.axis_size("chan") == 2
        and lax.axis_size("ctx") % 4 == 0
        and (batch, count) == (2, 3)
        and taps.shape[0] == rows
        and proj.shape[0] % 16 == 0
        and channels % 512 == 0
    ):
        return fused(value, gate_in, gate_out, filters, skip, proj, taps)
    tile = min(256, channels)
    consts = [jnp.asarray(t) for t in tables(rows)]
    gathered = lax.all_gather(proj, "ctx", axis=0, tiled=True)
    blocks = [value] + [from_behind(value, s) for s in range(1, count + 1)]
    mixed = tiled(
        mix_kernel, consts, [filters, skip[None]], [gate_in, *blocks], tile, 4 * 10**9
    )
    partial = mm(mixed.reshape(batch * rows, channels), gathered)
    groups = lax.axis_size("chan")
    me = lax.axis_index("chan")
    width = partial.shape[1] // groups

    def columns(owner):
        return lax.dynamic_slice_in_dim(partial, owner * width, width, axis=1)

    total = columns(me)
    for step in range(1, groups):
        pairs = [(s, (s + step) % groups) for s in range(groups)]
        total = total + lax.ppermute(
            columns((me + step) % groups).astype(BF16), "chan", pairs
        ).astype(F32)
    projected = total.astype(BF16).reshape(batch, rows, width)
    behind = from_behind(projected, 1)
    return tiled(filter_kernel, consts, [taps], [gate_out, behind, projected], tile, 2 * 10**9)


def solution(mesh):
    in_specs = (
        P(None, "ctx", "chan"),
        P(None, "ctx", "chan"),
        P(None, "ctx", "chan"),
        P(None, "chan"),
        P("chan"),
        P(("chan", "ctx"), None),
        P(None, "chan"),
    )
    out_specs = P(None, "ctx", "chan")
    return jax.shard_map(
        per_device, mesh=mesh, in_specs=in_specs, out_specs=out_specs, check_vma=False
    )
```

```python
import functools
import math

import jax
import jax.numpy as jnp
import numpy as np
from jax import lax
from jax.experimental import pallas as pl
from jax.experimental.pallas import tpu as pltpu
from jax.sharding import PartitionSpec as P

F32 = jnp.float32
BF16 = jnp.bfloat16


def split(x):
    high = x.astype(BF16)
    return high, (x - high.astype(F32)).astype(BF16)


def split_table(table):
    high = table.astype(BF16)
    return high, (table - high.astype(np.float64)).astype(BF16)


def tables(rows):
    size = 2 * rows
    product = (2 * np.arange(rows)[:, None] + 1) * np.arange(size)[None, :] % (2 * size)
    phase = product * (math.pi / size)
    forward = np.concatenate([np.cos(phase), -np.sin(phase)], axis=0)
    inverse = forward[:, rows:].T * (2.0 / size)
    return (*split_table(forward), *split_table(np.ascontiguousarray(inverse)))


def mm(left, right):
    return jnp.dot(left, right, preferred_element_type=F32)


def lag_spectrum(lags, fwd_hi, fwd_lo):
    rows = lags.shape[0]
    high, low = split(lags)
    return mm(fwd_hi[:, :rows], high) + mm(fwd_hi[:, :rows], low) + mm(fwd_lo[:, :rows], high)


def convolve(windows, spectra, table_refs):
    forward, inverse = table_refs[0], table_refs[2]
    total_re = total_im = None
    for window, spectrum in zip(windows, spectra):
        seen = mm(forward[...], window)
        half = seen.shape[0] // 2
        x_re, x_im, h_re, h_im = seen[:half], seen[half:], spectrum[:half], spectrum[half:]
        re = x_re * h_re - x_im * h_im
        im = x_re * h_im + x_im * h_re
        total_re = re if total_re is None else total_re + re
        total_im = im if total_im is None else total_im + im
    return mm(inverse[...], jnp.concatenate([total_re, total_im], axis=0).astype(BF16))


def mix_kernel(fh, fl, ih, il, filters, skip, gate, *rest):
    blocks, out = rest[:-1], rest[-1]
    batch, rows, _ = out.shape
    count = filters.shape[0] // rows
    spectra = [
        lag_spectrum(filters[s * rows : (s + 1) * rows], fh[...], fl[...]) for s in range(count)
    ]
    for b in range(batch):
        windows = [
            jnp.concatenate([blocks[s + 1][b], blocks[s][b]], axis=0) for s in range(count)
        ]
        conv = convolve(windows, spectra, (fh, fl, ih, il))
        own = blocks[0][b].astype(F32)
        out[b] = (gate[b].astype(F32) * (conv + skip[...] * own)).astype(BF16)


def filter_kernel(fh, fl, ih, il, taps, gate, behind, own, out):
    spectra = [lag_spectrum(taps[...], fh[...], fl[...])]
    for b in range(out.shape[0]):
        window = jnp.concatenate([behind[b], own[b]], axis=0)
        shorted = convolve([window], spectra, (fh, fl, ih, il))
        out[b] = (gate[b].astype(F32) * shorted).astype(BF16)


def tiled(kernel, consts, rows_args, block_args, tile, flops):
    batch, rows, channels = block_args[0].shape
    whole = lambda a: pl.BlockSpec(a.shape, lambda i: (0, 0))
    across = lambda a: pl.BlockSpec((a.shape[0], tile), lambda i: (0, i))
    block = pl.BlockSpec((batch, rows, tile), lambda i: (0, 0, i))
    args = [*consts, *rows_args, *block_args]
    return pl.pallas_call(
        kernel,
        grid=(channels // tile,),
        in_specs=[whole(a) for a in consts]
        + [across(a) for a in rows_args]
        + [block for _ in block_args],
        out_specs=block,
        out_shape=jax.ShapeDtypeStruct((batch, rows, channels), BF16),
        cost_estimate=pl.CostEstimate(
            flops=flops,
            bytes_accessed=sum(a.size * a.dtype.itemsize for a in args),
            transcendentals=0,
        ),
    )(*args)


def from_behind(value, steps):
    count = lax.axis_size("ctx")
    return lax.ppermute(value, "ctx", [(s, s + steps) for s in range(count - steps)])


MESH = pl.DeviceIdType.MESH


UNITS = 4


def fused_kernel(
    value_any, proj_any, fh_any, fl_any, ih_any, il_any, skip_any, filters_any, taps_any,
    gate_in_any, gate_out_any,
    out_any,
    value, fh, fl, ih, il, skip, out,
    past, gathered, mixed, spectra, tap_spectra, filters, taps, gate_in, gate_out,
    own_rows, rim,
    load_sem, store_sem, own_sem, back_send, back_recv, halo_send, halo_recv, relay_send, relay_recv, far_send, far_recv,
    near_send, near_recv, ring_send, ring_recv, share_send, share_recv, first_send, first_recv,
    swap_send, swap_recv, mixed_send, mixed_recv, rim_send, rim_recv,
):
    batch, rows, channels = value.shape
    count = lax.axis_size("ctx")
    chips = count // 2
    evens = chips // 2
    width = gathered.shape[-1]
    tile = min(256, width)
    me, j = lax.axis_index("chan"), lax.axis_index("ctx")
    chip, core = j // 2, j % 2
    sibling = chip * 2 + 1 - core
    partner = 1 - me
    place = jnp.where(chip % 2 == 0, chip // 2, chips - 1 - chip // 2)

    def holder(position):
        position = (position + chips) % chips
        number = jnp.where(position < evens, 2 * position, 2 * (chips - 1 - position) + 1)
        return number * 2 + core

    loads = [
        pltpu.make_async_copy(a, b, load_sem.at[i])
        for i, (a, b) in enumerate(
            [
                (filters_any, filters),
                (taps_any, taps),
                (gate_in_any, gate_in),
                (gate_out_any, gate_out),
                (fh_any, fh),
                (fl_any, fl),
                (ih_any, ih),
                (il_any, il),
                (skip_any, skip),
                (value_any, value),
            ]
        )
    ]
    for load in loads:
        load.start()

    def columns(owner, unit):
        return pl.ds(pl.multiple_of(owner * channels + unit * width, width), width)

    own_copies = [
        pltpu.make_async_copy(proj_any.at[:, columns(me, q)], gathered.at[q, me, j], own_sem.at[q])
        for q in range(UNITS)
    ]
    for copy in own_copies:
        copy.start()

    barrier = pltpu.get_barrier_semaphore()
    following, preceding = holder(place + 1), holder(place - 1)
    expected = 3
    for peer in ((me, following), (me, preceding), (partner, j)):
        pl.semaphore_signal(barrier, inc=1, device_id=peer, device_id_type=MESH)
    for offset in (-3, -2, -1, 1, 2, 3):
        there = (j + offset >= 0) & (j + offset < count)
        expected = expected + there.astype(jnp.int32)

        @pl.when(there)
        def _(offset=offset):
            pl.semaphore_signal(barrier, inc=1, device_id=(me, j + offset), device_id_type=MESH)

    pl.semaphore_wait(barrier, expected)

    def remote(source, target, send_sem, recv_sem, peer):
        return pltpu.make_async_remote_copy(
            src_ref=source,
            dst_ref=target,
            send_sem=send_sem,
            recv_sem=recv_sem,
            device_id=peer,
            device_id_type=MESH,
        )

    def halo(b):
        return remote(value_any.at[b], past.at[1, b], halo_send.at[b], halo_recv.at[b], (me, j + 2))

    def far(b):
        return remote(value_any.at[b], past.at[2, b], far_send.at[b], far_recv.at[b], (me, j + 3))

    def near(b):
        return remote(value_any.at[b], past.at[0, b], near_send.at[b], near_recv.at[b], (me, sibling))

    def relay(b, slot):
        return remote(
            past.at[1, b], past.at[slot, b], relay_send.at[b], relay_recv.at[b], (me, sibling)
        )

    def back(b):
        return remote(past.at[2, b], past.at[1, b], back_send.at[b], back_recv.at[b], (me, j - 1))

    first, second = core == 0, core == 1
    even, odd = chip % 2 == 0, chip % 2 == 1
    has_behind = j >= 2
    sends_halo, gets_halo = (j + 2 < count) & (even | first), (j >= 2) & (odd | first)
    sends_far, gets_far = second & (j + 3 < count), first & (j >= 3)
    sends_back, gets_back = first & odd & (j >= 3), second & even & (j >= 2)

    def start_halo(b):
        @pl.when(sends_far)
        def _():
            far(b).start()

        @pl.when(sends_halo)
        def _():
            halo(b).start()

        @pl.when(first)
        def _():
            near(b).start()

    sent = []

    def begin(copy):
        copy.start()
        sent.append(copy)

    reach = chips // 2

    def swap(unit):
        return remote(
            proj_any.at[:, columns(partner, unit)],
            gathered.at[unit, me, j],
            swap_send.at[unit],
            swap_recv.at[unit],
            (partner, j),
        )

    def piece(unit, direction, step, origin):
        if step < reach:
            return gathered.at[unit, :, origin]
        return gathered.at[unit, 0 if direction == 1 else 1, origin]

    def slot(direction, step):
        return step - 1 if direction == 1 else reach + step - 1

    def hop(unit, direction, step):
        origin = holder(place - direction * (step - 1))
        k = slot(direction, step)
        moved = piece(unit, direction, step, origin)
        return remote(
            moved,
            moved,
            ring_send.at[unit, k],
            ring_recv.at[unit, k],
            (me, following if direction == 1 else preceding),
        )

    def share(unit, direction, step, other=False):
        origin = holder(place - direction * step)
        if other:
            origin = origin + 1 - 2 * core
        k = slot(direction, step)
        moved = piece(unit, direction, step, origin)
        return remote(
            moved, moved, share_send.at[unit, k], share_recv.at[unit, k], (me, sibling)
        )

    def share_own(unit, other=False):
        moved = gathered.at[unit, :, sibling if other else j]
        return remote(moved, moved, first_send.at[unit], first_recv.at[unit], (me, sibling))

    hops = {}

    def wave(unit, step):
        if step == 1:
            own_copies[unit].wait()
            swaps[unit].wait_recv()
        for direction in (1, -1):
            if step > 1:
                hops[unit, direction, step - 1].wait_recv()
            if step <= reach:
                copy = hops[unit, direction, step] = hop(unit, direction, step)
                begin(copy)
        if step == 1:
            begin(share_own(unit))
        else:
            for direction in (1, -1):
                begin(share(unit, direction, step - 1))

    def finish(unit):
        share_own(unit, other=True).wait_recv()
        for direction in (1, -1):
            for step in range(1, reach + 1):
                share(unit, direction, step, other=True).wait_recv()

    def product(unit):
        total = None
        for plane in range(2):
            table = gathered[unit, plane].reshape(count * proj_any.shape[0], width)
            part = mm(mixed[plane].reshape(batch * rows, channels), table)
            total = part if total is None else total + part
        return total

    swaps = [swap(unit) for unit in range(UNITS)]
    for copy in swaps:
        begin(copy)
    start_halo(0)
    wave(0, 1)
    wave(1, 1)
    start_halo(1)
    wave(2, 1)
    wave(3, 1)
    waves = [(unit, step) for step in range(2, reach + 2) for unit in range(UNITS)]

    def pump(number):
        for _ in range(number):
            if waves:
                wave(*waves.pop(0))

    table_refs = (fh, fl, ih, il)
    for load in (loads[0], *loads[4:]):
        load.wait()

    @pl.loop(0, channels // tile)
    def _(i):
        at = pl.ds(pl.multiple_of(i * tile, tile), tile)
        for s in range(spectra.shape[0]):
            spectra[s, :, at] = lag_spectrum(filters[s * rows : (s + 1) * rows, at], fh[...], fl[...])

    @pl.when(j < 2)
    def _():
        past[1] = jnp.zeros(past.shape[1:], BF16)

    @pl.when((j < 2) & first)
    def _():
        past[0] = jnp.zeros(past.shape[1:], BF16)

    @pl.when((j < 2) & second | (j < 3) & first)
    def _():
        past[2] = jnp.zeros(past.shape[1:], BF16)

    def relay_halo(b):
        @pl.when(gets_far)
        def _():
            far(b).wait_recv()

        @pl.when(sends_back)
        def _():
            back(b).start()

        @pl.when(gets_halo)
        def _():
            halo(b).wait_recv()

        @pl.when(gets_back)
        def _():
            back(b).wait_recv()

        @pl.when(has_behind & first)
        def _():
            relay(b, 2).start()

        @pl.when(has_behind & second)
        def _():
            relay(b, 0).start()

    relay_halo(0)
    pump(2)
    relay_halo(1)
    pump(2)
    loads[2].wait()

    def mix(b):
        @pl.when(second)
        def _():
            near(b).wait_recv()

        @pl.when(has_behind & first)
        def _():
            relay(b, 0).wait_recv()

        @pl.when(has_behind & second)
        def _():
            relay(b, 2).wait_recv()

        @pl.loop(0, channels // tile)
        def _(i):
            at = pl.ds(pl.multiple_of(i * tile, tile), tile)
            parts = [value[b, :, at]] + [past[s, b, :, at] for s in range(3)]
            windows = [jnp.concatenate([parts[s + 1], parts[s]], axis=0) for s in range(3)]
            conv = convolve(windows, [spectra.at[s, :, at][...] for s in range(3)], table_refs)
            both = conv + skip[:, at] * parts[0].astype(F32)
            gated = gate_in[b, :, at].astype(F32) * both
            mixed[me, b, :, at] = gated.astype(BF16)

    def trade(b):
        return remote(
            mixed.at[me, b], mixed.at[me, b], mixed_send.at[b], mixed_recv.at[b], (partner, j)
        )

    def traded(b):
        moved = mixed.at[partner, b]
        return remote(moved, moved, mixed_send.at[b], mixed_recv.at[b], (partner, j))

    mix(0)
    begin(trade(0))
    pump(2)
    mix(1)
    begin(trade(1))
    pump(4)
    loads[1].wait()

    @pl.loop(0, channels // tile)
    def _(i):
        at = pl.ds(pl.multiple_of(i * tile, tile), tile)
        tap_spectra[:, at] = lag_spectrum(taps[:, at], fh[...], fl[...])

    @pl.when(j == 0)
    def _():
        rim[...] = jnp.zeros(rim.shape, BF16)

    loads[3].wait()

    def edge(u):
        return remote(
            own_rows.at[u], rim.at[u], rim_send.at[u], rim_recv.at[u], (me, j + 1)
        )

    def store(u):
        part = pl.ds(u * width, width)
        return pltpu.make_async_copy(
            out.at[:, :, part], out_any.at[:, :, part], store_sem.at[u]
        )

    def emit(u):
        @pl.when(j >= 1)
        def _():
            edge(u).wait_recv()

        wide = pl.ds(u * width, width)
        spectrum = tap_spectra[:, wide]
        for b in range(batch):
            window = jnp.concatenate([rim[u, b], own_rows[u, b]], axis=0)
            shorted = convolve([window], [spectrum], table_refs)
            out[b, :, wide] = (gate_out[b, :, wide].astype(F32) * shorted).astype(BF16)
        store(u).start()

    pump(len(waves))
    for u in range(UNITS):
        while any(w[0] == u for w in waves):
            pump(1)
        finish(u)
        if u == 0:
            for b in range(batch):
                traded(b).wait_recv()
        own_rows[u] = product(u).astype(BF16).reshape(batch, rows, width)

        @pl.when(j + 1 < count)
        def _(u=u):
            edge(u).start()

        if u:
            emit(u - 1)
    emit(UNITS - 1)

    for u in range(UNITS):
        store(u).wait()
    for copy in sent:
        copy.wait_send()

    for b in range(batch):

        @pl.when(sends_halo)
        def _(b=b):
            halo(b).wait_send()

        @pl.when(first)
        def _(b=b):
            near(b).wait_send()

        @pl.when(sends_far)
        def _(b=b):
            far(b).wait_send()

        @pl.when(has_behind)
        def _(b=b):
            relay(b, 0).wait_send()

        @pl.when(sends_back)
        def _(b=b):
            back(b).wait_send()

    for u in range(UNITS):

        @pl.when(j + 1 < count)
        def _(u=u):
            edge(u).wait_send()


def fused(value, gate_in, gate_out, filters, skip, proj, taps):
    batch, rows, channels = value.shape
    count = lax.axis_size("ctx")
    consts = [jnp.asarray(t) for t in tables(rows)]
    width = channels // UNITS
    slots = 2 * (count // 4)
    dma = pltpu.SemaphoreType.DMA
    anywhere = pl.BlockSpec(memory_space=pl.ANY)
    return pl.pallas_call(
        fused_kernel,
        out_shape=jax.ShapeDtypeStruct(value.shape, BF16),
        in_specs=[anywhere] * 11,
        out_specs=anywhere,
        scratch_shapes=[
            pltpu.VMEM(value.shape, BF16),
            *(pltpu.VMEM(t.shape, BF16) for t in consts),
            pltpu.VMEM((1, channels), F32),
            pltpu.VMEM(value.shape, BF16),
            pltpu.VMEM((3, batch, rows, channels), BF16),
            pltpu.VMEM((UNITS, 2, count, proj.shape[0], width), BF16),
            pltpu.VMEM((2, batch, rows, channels), BF16),
            pltpu.VMEM((3, 2 * rows, channels), F32),
            pltpu.VMEM((2 * rows, channels), F32),
            pltpu.VMEM(filters.shape, F32),
            pltpu.VMEM(taps.shape, F32),
            pltpu.VMEM(value.shape, BF16),
            pltpu.VMEM(value.shape, BF16),
            pltpu.VMEM((UNITS, batch, rows, width), BF16),
            pltpu.VMEM((UNITS, batch, rows, width), BF16),
            dma((10,)),
            dma((UNITS,)),
            dma((UNITS,)),
            dma((batch,)),
            dma((batch,)),
        ]
        + [dma((batch,))] * 8
        + [dma((UNITS, slots))] * 4
        + [dma((UNITS,))] * 4
        + [dma((batch,))] * 2
        + [dma((UNITS,))] * 2,
        compiler_params=pltpu.CompilerParams(
            collective_id=0, has_side_effects=True, vmem_limit_bytes=67043328
        ),
    )(value, proj, *consts, skip[None], filters, taps, gate_in, gate_out)


def per_device(value, gate_in, gate_out, filters, skip, proj, taps):
    batch, rows, channels = value.shape
    assert filters.shape[0] % rows == 0 and taps.shape[0] <= rows
    count = filters.shape[0] // rows
    if (
        lax.axis_size("chan") == 2
        and lax.axis_size("ctx") % 4 == 0
        and (batch, count) == (2, 3)
        and taps.shape[0] == rows
        and proj.shape[0] % 16 == 0
        and channels % 512 == 0
    ):
        return fused(value, gate_in, gate_out, filters, skip, proj, taps)
    tile = min(256, channels)
    consts = [jnp.asarray(t) for t in tables(rows)]
    gathered = lax.all_gather(proj, "ctx", axis=0, tiled=True)
    blocks = [value] + [from_behind(value, s) for s in range(1, count + 1)]
    mixed = tiled(
        mix_kernel, consts, [filters, skip[None]], [gate_in, *blocks], tile, 4 * 10**9
    )
    partial = mm(mixed.reshape(batch * rows, channels), gathered)
    groups = lax.axis_size("chan")
    me = lax.axis_index("chan")
    width = partial.shape[1] // groups

    def columns(owner):
        return lax.dynamic_slice_in_dim(partial, owner * width, width, axis=1)

    total = columns(me)
    for step in range(1, groups):
        pairs = [(s, (s + step) % groups) for s in range(groups)]
        total = total + lax.ppermute(
            columns((me + step) % groups).astype(BF16), "chan", pairs
        ).astype(F32)
    projected = total.astype(BF16).reshape(batch, rows, width)
    behind = from_behind(projected, 1)
    return tiled(filter_kernel, consts, [taps], [gate_out, behind, projected], tile, 2 * 10**9)


def solution(mesh):
    in_specs = (
        P(None, "ctx", "chan"),
        P(None, "ctx", "chan"),
        P(None, "ctx", "chan"),
        P(None, "chan"),
        P("chan"),
        P(("chan", "ctx"), None),
        P(None, "chan"),
    )
    out_specs = P(None, "ctx", "chan")
    return jax.shard_map(
        per_device, mesh=mesh, in_specs=in_specs, out_specs=out_specs, check_vma=False
    )
```
